128 devices in a mesh: lat: 32 (over z, y, core), tp: 4 (over x).
Axes of the slice: x: 4, y: 4, z: 4, core: 2. Of those that a mesh axis runs over, the one named last changes fastest.
Arguments:
- activations: bfloat16 [8192, 7168], P('lat', 'tp'), may hold values from -16 to 16, as said below
- active_blocks: int32 [8192, 2], P('lat'), may hold values from 0 to 31, all different within a row; in each aligned block of 256 rows (0 to 255, 256 to 511, ...) at most 32 rows name the same one
- enc_weight: bfloat16 [7168, 65536], P('tp', 'lat'), may hold values from -0.0625 to 0.0625
- enc_bias: float32 [65536], P('lat'), may hold values from -3 to 3
- dec_weight: bfloat16 [65536, 7168], P('lat', 'tp'), may hold values from -0.125 to 0.125
- dec_bias: float32 [7168], P('tp'), may hold values from -3 to 3
Outputs:
- token_error: float32 [8192], P('lat')
- mean_error: float32 [], replicated
The draws below stay inside these ranges and needn't reach their ends.
Inputs may be any that keep to these rules, and one draw needn't show every extreme that they name: `active_blocks`: each row names 2 different blocks; among the rows of one index of lat no block is named more than 32 times, and some block is named exactly 32 times. `activations`: real values.
All inputs are finite; a program needn't handle non-finite values.
Results may differ from the reference program's by a relative error of at most 0.005.
Values may be sent and summed in bfloat16 or wider, within the bound.
No kernel may reach another device: no remote copies, remote signals or barrier semaphores. Data moves between devices by JAX's collectives and lax.ppermute only.
A program may use at most 64 MiB of HBM per device.

```python
import math
import jax
import jax.numpy as jnp
import numpy as np
from jax import lax

D = 7168
BLOCK = 2048
K_ACT = 2
TOK_DEV = 256
TOKENS = 8192
LATENTS = 65536
CAP = 32
N_LAT = 32
N_TP = 4


def draw_activations(key, part):
    position = jnp.arange(TOKENS, dtype=jnp.float32) / TOKENS
    row_scale = 0.25 * jnp.exp(position * jnp.log(10.0))
    values = jnp.clip(jax.random.normal(key, (TOKENS, D), jnp.float32), -6.0, 6.0)
    return (values * row_scale[:, None]).astype(jnp.bfloat16)


def levels(own_key, dims, shards, low, top_value):
    level = 1.0
    for dim, blocks in shards:
        steps = jax.random.uniform(jax.random.fold_in(jax.random.fold_in(own_key, 6), dim), (blocks,), jnp.float32, low / len(shards), top_value / len(shards))
        level = level * jnp.repeat(jnp.exp(steps), dims[dim] // blocks).reshape((-1,) + (1,) * (len(dims) - 1 - dim))
    return level


def deal_out(rng, own, number, rows, number_of, top, most, lean):
    sequence = jax.random.permutation(rng, number_of)
    crowded, common = portions_of(number_of, rows * top, most, lean, True), portions_of(number_of, rows * top, most, lean, False)
    places = jnp.arange(number_of)

    def named(sizes, offset_by):
        used = int((sizes > 0).sum())
        fixed = max(1, used // 4)
        shifted = fixed + (places - fixed + offset_by * (used - fixed)) % max(1, number_of - fixed)
        return jnp.zeros((number_of,), jnp.int32).at[sequence[jnp.where(places < fixed, places, shifted)]].set(jnp.asarray(sizes, jnp.int32))

    sizes = jnp.where(number % 4 == 0, named(crowded, number // 4), named(common, number - number // 4 - 1))
    mixed = jax.random.permutation(jax.random.fold_in(own, 3), number_of)
    donor, taker = mixed[0:number_of // 2 * 2:2], mixed[1:number_of // 2 * 2:2]
    slack = jnp.minimum(sizes[donor] - 1, most - sizes[taker]) // 2
    slack = jnp.where((donor == sequence[0]) | (taker == sequence[0]) | (sizes[taker] == 0), 0, jnp.maximum(slack, 0))
    shifted = jax.random.randint(jax.random.fold_in(own, 4), (number_of // 2,), 0, 1 << 20) % (slack + 1)
    sizes = sizes.at[donor].add(-shifted).at[taker].add(shifted)
    items = jnp.searchsorted(jnp.cumsum(sizes), jnp.arange(rows * top), side="right").astype(jnp.int32)
    table = items.reshape(top, rows).T
    table = table[jax.random.permutation(jax.random.fold_in(own, 1), rows)]
    offset_by = jax.random.randint(jax.random.fold_in(own, 2), (rows, 1), 0, top)
    return jnp.take_along_axis(table, (jnp.arange(top)[None, :] + offset_by) % top, axis=1)


def portions_of(count, total, most, skew, full):
    loads = [(1 << 20) // math.isqrt(rank ** skew) + 1 for rank in range(1, count + 1)]
    largest = most if full else min(most, max(-(-total // count), total * loads[0] // sum(loads)))
    least = 1 if total - largest >= count - 1 else 0
    holding, rest = [largest] + [least] * (count - 1), total - largest - least * (count - 1)
    while rest > 0:
        movable = [i for i in range(1, count) if holding[i] < largest] or [i for i in range(1, count) if holding[i] < most]
        pool, remaining = sum([loads[i] for i in movable]), rest
        for i in movable:
            extra = min(most - holding[i], max(1, remaining * loads[i] // pool), rest)
            holding[i] = holding[i] + extra
            rest = rest - extra
    return np.array(holding)


def gaussian(stream_key, dims, deviation, most, split=(), kind=jnp.bfloat16):
    array = deviation * jax.random.normal(stream_key, dims, jnp.float32)
    if split:
        array = array * levels(stream_key, dims, split, -0.22, 0.18)
    return jnp.clip(array, -most, most).astype(kind)


def setup_inputs(seed: int = 0) -> dict:
    seeds = jax.random.split(jax.random.key(seed), 7)
    activations = draw_activations(jax.random.fold_in(seeds[6], 71), 0)
    active_blocks_keys = jax.random.split(jax.random.fold_in(seeds[1], 1), TOKENS // TOK_DEV)
    active_blocks_turns = jax.random.permutation(jax.random.fold_in(seeds[1], 3), TOKENS // TOK_DEV)
    active_blocks = jax.vmap(lambda own, number: deal_out(jax.random.fold_in(seeds[1], 2), own, number, TOK_DEV, N_LAT, K_ACT, CAP, 2))(active_blocks_keys, active_blocks_turns).reshape((TOKENS, K_ACT))
    enc_weight = gaussian(seeds[2], (D, LATENTS), D ** -0.5, 0.0625, ((0, 4), (1, 32)))
    enc_bias = gaussian(seeds[3], (LATENTS,), 0.5, 3.0, ((0, 32),), jnp.float32)
    dec_weight = gaussian(seeds[4], (LATENTS, D), BLOCK ** -0.5, 0.125, ((0, 32), (1, 4)))
    dec_bias = gaussian(seeds[5], (D,), 0.5, 3.0, ((0, 4),), jnp.float32)
    return {"activations": activations, "active_blocks": active_blocks, "enc_weight": enc_weight, "enc_bias": enc_bias, "dec_weight": dec_weight, "dec_bias": dec_bias}


def reference(activations, active_blocks, enc_weight, enc_bias, dec_weight, dec_bias):
    width = activations.shape[1]
    part_width = width // N_TP
    centred = (activations.astype(jnp.float32) - dec_bias).astype(jnp.bfloat16)
    flat = active_blocks.reshape(-1).astype(jnp.int32)
    slots = CAP * N_LAT
    order = jnp.argsort(flat, stable=True).astype(jnp.int32)
    order = jnp.concatenate([order, jnp.zeros((slots,), jnp.int32)])
    counts = jnp.sum((flat[:, None] == jnp.arange(N_LAT, dtype=jnp.int32)[None, :]).astype(jnp.int32), axis=0)
    starts = (jnp.cumsum(counts) - counts).astype(jnp.int32)

    def one_block(index, total):
        picked = lax.dynamic_slice_in_dim(order, starts[index], slots)
        rows_of = (picked // K_ACT).astype(jnp.int32)
        valid = (jnp.arange(slots, dtype=jnp.int32) < counts[index]).astype(jnp.float32)
        inputs = centred[rows_of].reshape(slots, N_TP, part_width).astype(jnp.float32)
        w_enc = lax.dynamic_slice_in_dim(enc_weight, index * BLOCK, BLOCK, 1)
        w_enc = w_enc.reshape(N_TP, part_width, BLOCK).astype(jnp.float32)
        parts = jnp.einsum('rtd,tdl->rtl', inputs, w_enc)
        parts = lax.optimization_barrier(parts.astype(jnp.bfloat16)).astype(jnp.float32)
        bias = lax.dynamic_slice_in_dim(enc_bias, index * BLOCK, BLOCK)
        pre = jnp.sum(parts, axis=1) + bias
        latents = jnp.maximum(pre, 0.0).astype(jnp.bfloat16)
        w_dec = lax.dynamic_slice_in_dim(dec_weight, index * BLOCK, BLOCK, 0)
        decoded = jnp.dot(latents, w_dec, preferred_element_type=jnp.float32).astype(jnp.bfloat16)
        decoded = decoded.astype(jnp.float32) * valid[:, None]
        return total.at[rows_of].add(decoded)

    start_total = jnp.zeros(activations.shape, jnp.float32)
    summed = lax.fori_loop(0, N_LAT, one_block, start_total)
    recon = summed + dec_bias
    inputs_full = activations.astype(jnp.float32)
    diff = inputs_full - recon
    token_error = jnp.sum(diff * diff, axis=1) / (jnp.sum(inputs_full * inputs_full, axis=1) + 1e-6)
    mean_error = jnp.sum(token_error) / TOKENS
    return token_error, mean_error
```

```python
import jax
import jax.numpy as jnp
from jax import lax
from jax.experimental import pallas as pl
from jax.experimental.pallas import tpu as pltpu
from jax.sharding import PartitionSpec as P


AXES = ("lat", "tp")
N_Z, N_Y, N_C, N_X = 4, 4, 2, 4
TOK = 256
WIDTH = 1792
BLOCK = 2048
SLOTS = 32
PACKED = TOK + 16
PIECE = N_C * SLOTS
ROWS = N_Y * PIECE


def split_index(index):
    x = index % N_X
    lat = index // N_X
    return lat // (N_Y * N_C), (lat // N_C) % N_Y, lat % N_C, x


def pairs(change):
    out = []
    for index in range(N_Z * N_Y * N_C * N_X):
        z, y, c, x = change(*split_index(index))
        out.append((index, ((z * N_Y + y) * N_C + c) * N_X + x))
    return out


def first(c):
    return 1 + 2 * c


def second(c):
    return 3 - 2 * c


TO_CORE = pairs(lambda z, y, c, x: (z, y, 1 - c, x))
TO_Y = {d: pairs(lambda z, y, c, x, d=d: (z, y ^ d, c, x)) for d in (1, 2, 3)}
TO_ZA = pairs(lambda z, y, c, x: (z ^ first(c), y, c, x))
TO_ZB = pairs(lambda z, y, c, x: (z ^ second(c), y, c, x))
TO_ZC = pairs(lambda z, y, c, x: (z ^ 2, y, c, x))
TO_XA = pairs(lambda z, y, c, x: (z, y, c, x ^ first(c)))
TO_XB = pairs(lambda z, y, c, x: (z, y, c, x ^ second(c)))
TO_Z1 = pairs(lambda z, y, c, x: (z ^ 1, y, c, x))
TO_Z3 = pairs(lambda z, y, c, x: (z ^ 3, y, c, x))
TO_X1 = pairs(lambda z, y, c, x: (z, y, c, x ^ 1))
TO_X3 = pairs(lambda z, y, c, x: (z, y, c, x ^ 3))


def send(value, table):
    return lax.ppermute(value, AXES, table)


def smem():
    return pl.BlockSpec(memory_space=pltpu.SMEM)


def cost(flops, moved):
    return pl.CostEstimate(flops=flops, transcendentals=0, bytes_accessed=moved)


def lane_sums(values):
    acc = values[:, :128]
    for start in range(128, values.shape[1], 128):
        acc = acc + values[:, start:start + 128]
    return jnp.sum(acc.T, axis=0, keepdims=True)


def pack_kernel(act_ref, ids_ref, bias_ref, out_ref, norm_ref):
    values = act_ref[...].astype(jnp.float32)
    out_ref[0:TOK, :] = (values - bias_ref[...]).astype(jnp.bfloat16)
    norm_ref[...] = lane_sums(values * values)
    owners = N_Z * N_Y * N_C
    block = lax.broadcasted_iota(jnp.int32, (owners, TOK), 0)
    hot0 = ids_ref[0:1, :] == block
    hot1 = ids_ref[1:2, :] == block
    one0 = jnp.where(hot0, 1.0, 0.0)
    one1 = jnp.where(hot1, 1.0, 0.0)
    before = lax.broadcasted_iota(jnp.int32, (TOK, TOK), 0) < lax.broadcasted_iota(jnp.int32, (TOK, TOK), 1)
    before = jnp.where(before, 1.0, 0.0).astype(jnp.bfloat16)
    count0 = jnp.dot(one0.astype(jnp.bfloat16), before, preferred_element_type=jnp.float32)
    count1 = jnp.dot(one1.astype(jnp.bfloat16), before, preferred_element_type=jnp.float32)
    count1 = count1 + jnp.sum(one0, axis=1, keepdims=True)
    rank0 = jnp.sum(one0 * count0, axis=0, keepdims=True)
    rank1 = jnp.sum(one1 * count1, axis=0, keepdims=True)
    name0 = ids_ref[0:1, :].astype(jnp.float32)
    name1 = ids_ref[1:2, :].astype(jnp.float32)
    table = jnp.concatenate([name0, name1, rank0, rank1, jnp.zeros((12, TOK), jnp.float32)], axis=0)
    out_ref[TOK:PACKED, 0:TOK] = table.astype(jnp.bfloat16)
    out_ref[TOK:PACKED, TOK:WIDTH] = jnp.zeros((16, WIDTH - TOK), jnp.bfloat16)


def pack(activations, ids, dec_bias):
    return pl.pallas_call(
        pack_kernel,
        out_shape=(
            jax.ShapeDtypeStruct((PACKED, WIDTH), jnp.bfloat16),
            jax.ShapeDtypeStruct((1, TOK), jnp.float32),
        ),
        cost_estimate=cost(2**24, 4 * TOK * WIDTH),
        name="pack",
    )(activations, ids, dec_bias)


def place(meta, table, row_count=N_Y * SLOTS):
    index = meta[0]
    lat = index // N_X
    z, y, c = lat // (N_Y * N_C), (lat // N_C) % N_Y, lat % N_C
    row = lax.broadcasted_iota(jnp.int32, (row_count, 1), 0)
    owner = (z * N_Y + (y ^ (row // SLOTS))) * N_C + c
    want = (owner * SLOTS + row % SLOTS).astype(jnp.float32)
    table = table.astype(jnp.float32)
    code0 = table[0:1, :] * SLOTS + table[2:3, :]
    code1 = table[1:2, :] * SLOTS + table[3:4, :]
    hit = (code0 == want) | (code1 == want)
    return jnp.where(hit, 1.0, 0.0).astype(jnp.bfloat16)


def gather_kernel(meta_ref, own_ref, other_ref, *out_refs):
    for source, ref in enumerate((own_ref, other_ref)):
        picks = place(meta_ref, ref[TOK:PACKED, 0:TOK])
        rows = jnp.dot(picks, ref[0:TOK, :], preferred_element_type=jnp.float32).astype(jnp.bfloat16)
        for d, out_ref in enumerate(out_refs):
            out_ref[source * SLOTS:(source + 1) * SLOTS, :] = rows[d * SLOTS:(d + 1) * SLOTS, :]


def gather(meta, own, other):
    vmem = pl.BlockSpec((PACKED, WIDTH), lambda i: (0, 0))
    return pl.pallas_call(
        gather_kernel,
        grid=(1,),
        out_specs=[pl.BlockSpec((PIECE, WIDTH), lambda i: (0, 0))] * N_Y,
        in_specs=[smem(), vmem, vmem],
        out_shape=[jax.ShapeDtypeStruct((PIECE, WIDTH), jnp.bfloat16)] * N_Y,
        cost_estimate=cost(2 * 2 * 128 * TOK * WIDTH, 6 * TOK * WIDTH),
        name="gather",
    )(meta, own, other)


def scatter_kernel(meta_ref, own_ref, other_ref, *refs):
    pieces, outs = refs[:N_Y], refs[N_Y:]
    for source, (ref, out_ref) in enumerate(zip((own_ref, other_ref), outs)):
        picks = place(meta_ref, ref[:, 0:TOK])
        rows = jnp.concatenate([piece[source * SLOTS:(source + 1) * SLOTS, :] for piece in pieces], axis=0)
        total = lax.dot_general(picks, rows, (((0,), (0,)), ((), ())), preferred_element_type=jnp.float32)
        out_ref[...] = total.astype(jnp.bfloat16)


def scatter(meta, own, other, pieces):
    table = pl.BlockSpec((16, WIDTH), lambda i: (TOK // 16, 0))
    piece = pl.BlockSpec((PIECE, WIDTH), lambda i: (0, 0))
    return pl.pallas_call(
        scatter_kernel,
        grid=(1,),
        in_specs=[smem(), table, table] + [piece] * N_Y,
        out_specs=[pl.BlockSpec((TOK, WIDTH), lambda i: (0, 0))] * 2,
        out_shape=[jax.ShapeDtypeStruct((TOK, WIDTH), jnp.bfloat16)] * 2,
        cost_estimate=cost(2 * 2 * 128 * TOK * WIDTH, 6 * TOK * WIDTH),
        name="scatter",
    )(meta, own, other, *pieces)


def position(meta, quarter):
    index = meta[0]
    x, c = index % N_X, (index // N_X) % N_C
    d = x ^ quarter
    return jnp.where(d == 0, 0, jnp.where(d == second(c), 1, jnp.where(d == first(c), 2, 3)))


def encode_kernel(meta_ref, *refs):
    pieces = refs[:N_Y]
    weight_ref, own_ref, near_ref, away_ref, rows_ref = refs[N_Y:]

    @pl.when(pl.program_id(0) == 0)
    def _():
        for quarter, piece in enumerate(pieces):
            start = pl.multiple_of(position(meta_ref, quarter) * PIECE, PIECE)
            rows_ref[pl.ds(start, PIECE), :] = piece[...]

    part = jnp.dot(rows_ref[...], weight_ref[...], preferred_element_type=jnp.float32).astype(jnp.bfloat16)
    own_ref[...] = part[0:PIECE]
    near_ref[...] = part[PIECE:2 * PIECE]
    away_ref[...] = part[2 * PIECE:]


def encode(meta, pieces, weight, tile=512):
    piece = pl.BlockSpec((PIECE, WIDTH), lambda j: (0, 0))
    return pl.pallas_call(
        encode_kernel,
        grid=(BLOCK // tile,),
        in_specs=[smem()] + [piece] * N_Y + [pl.BlockSpec((WIDTH, tile), lambda j: (0, j))],
        out_specs=[
            pl.BlockSpec((PIECE, tile), lambda j: (0, j)),
            pl.BlockSpec((PIECE, tile), lambda j: (0, j)),
            pl.BlockSpec((2 * PIECE, tile), lambda j: (0, j)),
        ],
        out_shape=[
            jax.ShapeDtypeStruct((PIECE, BLOCK), jnp.bfloat16),
            jax.ShapeDtypeStruct((PIECE, BLOCK), jnp.bfloat16),
            jax.ShapeDtypeStruct((2 * PIECE, BLOCK), jnp.bfloat16),
        ],
        scratch_shapes=[pltpu.VMEM((ROWS, WIDTH), jnp.bfloat16)],
        cost_estimate=cost(2 * ROWS * WIDTH * BLOCK, 2 * WIDTH * BLOCK),
        name="encode",
    )(meta, *pieces, weight)


def decode_kernel(meta_ref, pair_ref, away_ref, weight_ref, *refs):
    outs, rows_ref, full_ref = refs[:N_Y], refs[N_Y], refs[N_Y + 1]

    @pl.when(pl.program_id(0) == 0)
    def _():
        rows_ref[0:2 * PIECE, :] = pair_ref[...]
        rows_ref[2 * PIECE:, :] = away_ref[...]

    full_ref[...] = jnp.dot(rows_ref[...], weight_ref[...], preferred_element_type=jnp.float32).astype(jnp.bfloat16)
    for quarter, out_ref in enumerate(outs):
        start = pl.multiple_of(position(meta_ref, quarter) * PIECE, PIECE)
        out_ref[...] = full_ref[pl.ds(start, PIECE), :]


def decode(meta, pair, away, weight, tile=256):
    half = pl.BlockSpec((2 * PIECE, BLOCK), lambda j: (0, 0))
    return pl.pallas_call(
        decode_kernel,
        grid=(WIDTH // tile,),
        in_specs=[smem(), half, half, pl.BlockSpec((BLOCK, tile), lambda j: (0, j))],
        out_specs=[pl.BlockSpec((PIECE, tile), lambda j: (0, j))] * N_Y,
        out_shape=[jax.ShapeDtypeStruct((PIECE, WIDTH), jnp.bfloat16)] * N_Y,
        scratch_shapes=[pltpu.VMEM((ROWS, BLOCK), jnp.bfloat16), pltpu.VMEM((ROWS, tile), jnp.bfloat16)],
        cost_estimate=cost(2 * ROWS * WIDTH * BLOCK, 2 * WIDTH * BLOCK),
        name="decode",
    )(meta, pair, away, weight)


def finish_kernel(act_ref, bias_ref, *refs):
    parts, out_ref = refs[:-1], refs[-1]
    recon = parts[0][...].astype(jnp.float32)
    for part in parts[1:]:
        recon = recon + part[...].astype(jnp.float32)
    diff = act_ref[...].astype(jnp.float32) - (recon + bias_ref[...])
    out_ref[...] = lane_sums(diff * diff)


def finish(activations, dec_bias, parts):
    return pl.pallas_call(
        finish_kernel,
        out_shape=jax.ShapeDtypeStruct((1, TOK), jnp.float32),
        cost_estimate=cost(2**22, 12 * TOK * WIDTH),
        name="finish",
    )(activations, dec_bias, *parts)


def sum_tp(value):
    value = value + send(value, TO_X1)
    return value + send(value, TO_X3)


def body(activations, active_blocks, enc_weight, enc_bias, dec_weight, dec_bias):
    meta = (lax.axis_index("lat") * N_X + lax.axis_index("tp")).astype(jnp.int32).reshape(1)
    bias_row = dec_bias.reshape(1, WIDTH)
    packed, norm = pack(activations, active_blocks.T, bias_row)

    from_a = send(packed, TO_ZA)
    late, from_a = lax.optimization_barrier((packed, from_a))
    from_c = send(from_a, TO_ZB)
    from_b = send(late, TO_ZB)
    norms = sum_tp(norm) + 1e-6

    def forward(own):
        other = send(own, TO_CORE)
        pieces = gather(meta, own, other)
        pieces = [pieces[0]] + [send(pieces[d], TO_Y[d]) for d in (1, 2, 3)]
        own_part, near_part, away_part = encode(meta, pieces, enc_weight)
        got = send(away_part, TO_XA)
        near_sum = (near_part.astype(jnp.float32) + got[PIECE:].astype(jnp.float32)).astype(jnp.bfloat16)
        rest = send(near_sum, TO_XB)
        pre = own_part.astype(jnp.float32) + got[:PIECE].astype(jnp.float32) + rest.astype(jnp.float32)
        mine = jnp.maximum(pre + enc_bias, 0.0).astype(jnp.bfloat16)
        near = send(mine, TO_XB)
        pair = jnp.concatenate([mine, near], axis=0)
        away = send(pair, TO_XA)
        back = decode(meta, pair, away, dec_weight)
        back = [back[0]] + [send(back[d], TO_Y[d]) for d in (1, 2, 3)]
        mine_total, other_total = scatter(meta, own, other, back)
        return mine_total, send(other_total, TO_CORE)

    def merged(parts):
        return (parts[0].astype(jnp.float32) + parts[1].astype(jnp.float32)).astype(jnp.bfloat16)

    home = list(forward(packed))
    home.append(send(merged(forward(from_a)), TO_ZA))
    home.append(send(merged(forward(from_c)), TO_ZC))
    home.append(send(merged(forward(from_b)), TO_ZB))

    squares = sum_tp(finish(activations, bias_row, home))
    token_error = (squares / norms).reshape(TOK)
    total = token_error[:128] + token_error[128:]
    for table in (TO_CORE, TO_Y[1], TO_Y[3], TO_Z1, TO_Z3):
        total = total + send(total, table)
    mean_error = jnp.sum(total) / (TOK * N_Z * N_Y * N_C)
    return (token_error, mean_error)


def solution(mesh):
    in_specs = (P("lat", "tp"), P("lat", None), P("tp", "lat"), P("lat"), P("lat", "tp"), P("tp"))
    out_specs = (P("lat"), P())
    return jax.shard_map(body, mesh=mesh, in_specs=in_specs, out_specs=out_specs, check_vma=False)
```

```python
import jax
import jax.numpy as jnp
from jax import lax
from jax.experimental import pallas as pl
from jax.experimental.pallas import tpu as pltpu
from jax.sharding import PartitionSpec as P


AXES = ("lat", "tp")
N_Z, N_Y, N_C, N_X = 4, 4, 2, 4
OWNERS = N_Z * N_Y * N_C
TOK = 256
WIDTH = 1792
BLOCK = 2048
SLOTS = 32
CHUNKS = 2
PART = SLOTS // CHUNKS
ROWS = OWNERS * PART
QUARTER = ROWS // N_X

def split_index(index):
    x = index % N_X
    lat = index // N_X
    return lat // (N_Y * N_C), (lat // N_C) % N_Y, lat % N_C, x


def pairs(change):
    out = []
    for index in range(N_Z * N_Y * N_C * N_X):
        z, y, c, x = change(*split_index(index))
        out.append((index, ((z * N_Y + y) * N_C + c) * N_X + x))
    return out


def first(c):
    return 1 + 2 * c


def second(c):
    return 3 - 2 * c


TO_XA = pairs(lambda z, y, c, x: (z, y, c, x ^ first(c)))
TO_XB = pairs(lambda z, y, c, x: (z, y, c, x ^ second(c)))
TO_X1 = pairs(lambda z, y, c, x: (z, y, c, x ^ 1))
TO_X3 = pairs(lambda z, y, c, x: (z, y, c, x ^ 3))
TO_LAT = [
    pairs(lambda z, y, c, x: (z, y, 1 - c, x)),
    pairs(lambda z, y, c, x: (z, y ^ 1, c, x)),
    pairs(lambda z, y, c, x: (z, y ^ 3, c, x)),
    pairs(lambda z, y, c, x: (z ^ 1, y, c, x)),
    pairs(lambda z, y, c, x: (z ^ 3, y, c, x)),
]

def send(value, table):
    return lax.ppermute(value, AXES, table)


def smem():
    return pl.BlockSpec(memory_space=pltpu.SMEM)


def cost(flops, moved):
    return pl.CostEstimate(flops=flops, transcendentals=0, bytes_accessed=moved)


def lane_sums(values):
    acc = values[:, :128]
    for start in range(128, values.shape[1], 128):
        acc = acc + values[:, start:start + 128]
    return jnp.sum(acc.T, axis=0, keepdims=True)


def code_kernel(ids_ref, code_ref):
    block = lax.broadcasted_iota(jnp.int32, (OWNERS, TOK), 0)
    one0 = jnp.where(ids_ref[0:1, :] == block, 1.0, 0.0)
    one1 = jnp.where(ids_ref[1:2, :] == block, 1.0, 0.0)
    before = lax.broadcasted_iota(jnp.int32, (TOK, TOK), 0) < lax.broadcasted_iota(jnp.int32, (TOK, TOK), 1)
    before = jnp.where(before, 1.0, 0.0).astype(jnp.bfloat16)
    count0 = jnp.dot(one0.astype(jnp.bfloat16), before, preferred_element_type=jnp.float32)
    count1 = jnp.dot(one1.astype(jnp.bfloat16), before, preferred_element_type=jnp.float32)
    count1 = count1 + jnp.sum(one0, axis=1, keepdims=True)
    rank0 = jnp.sum(one0 * count0, axis=0, keepdims=True)
    rank1 = jnp.sum(one1 * count1, axis=0, keepdims=True)
    code_ref[0:1, :] = ids_ref[0:1, :] * SLOTS + rank0.astype(jnp.int32)
    code_ref[1:2, :] = ids_ref[1:2, :] * SLOTS + rank1.astype(jnp.int32)


def codes(ids):
    return pl.pallas_call(
        code_kernel, out_shape=jax.ShapeDtypeStruct((2, TOK), jnp.int32), cost_estimate=cost(2**24, 2**13), name="codes"
    )(ids)


def picks(code_ref, chunk):
    row = lax.broadcasted_iota(jnp.int32, (ROWS, 1), 0)
    want = row // PART * SLOTS + chunk * PART + row % PART
    hit = (code_ref[0:1, :] == want) | (code_ref[1:2, :] == want)
    return jnp.where(hit, 1.0, 0.0).astype(jnp.bfloat16)


def pack_kernel(chunk, act_ref, code_ref, bias_ref, out_ref):
    centred = (act_ref[...].astype(jnp.float32) - bias_ref[...]).astype(jnp.bfloat16)
    rows = jnp.dot(picks(code_ref, chunk), centred, preferred_element_type=jnp.float32)
    out_ref[...] = rows.astype(jnp.bfloat16)


def pack(chunk, activations, code, dec_bias):
    return pl.pallas_call(
        lambda *refs: pack_kernel(chunk, *refs),
        out_shape=jax.ShapeDtypeStruct((ROWS, WIDTH), jnp.bfloat16),
        cost_estimate=cost(2 * ROWS * TOK * WIDTH, 2 * (ROWS + TOK) * WIDTH),
        name="pack",
    )(activations, code, dec_bias)


def norm_kernel(act_ref, out_ref):
    values = act_ref[...].astype(jnp.float32)
    out_ref[...] = lane_sums(values * values)


def norm_sums(activations):
    return pl.pallas_call(
        norm_kernel,
        out_shape=jax.ShapeDtypeStruct((1, TOK), jnp.float32),
        cost_estimate=cost(2**20, 2 * TOK * WIDTH),
        name="norms",
    )(activations)


def quarters(meta):
    index = meta[0]
    x, c = index % N_X, (index // N_X) % N_C
    return [pl.multiple_of((x ^ d) * QUARTER, QUARTER) for d in (0, second(c), first(c), 2)]


def encode_kernel(meta_ref, rows_ref, weight_ref, own_ref, near_ref, away_ref, part_ref):
    part_ref[...] = jnp.dot(rows_ref[...], weight_ref[...], preferred_element_type=jnp.float32).astype(jnp.bfloat16)
    own, near, away, far = quarters(meta_ref)
    own_ref[...] = part_ref[pl.ds(own, QUARTER), :]
    near_ref[...] = part_ref[pl.ds(near, QUARTER), :]
    away_ref[0:QUARTER, :] = part_ref[pl.ds(away, QUARTER), :]
    away_ref[QUARTER:, :] = part_ref[pl.ds(far, QUARTER), :]


def encode(meta, rows, weight, tile=512):
    out = pl.BlockSpec((QUARTER, tile), lambda j: (0, j))
    return pl.pallas_call(
        encode_kernel,
        grid=(BLOCK // tile,),
        in_specs=[smem(), pl.BlockSpec((ROWS, WIDTH), lambda j: (0, 0)), pl.BlockSpec((WIDTH, tile), lambda j: (0, j))],
        out_specs=[out, out, pl.BlockSpec((2 * QUARTER, tile), lambda j: (0, j))],
        out_shape=[
            jax.ShapeDtypeStruct((QUARTER, BLOCK), jnp.bfloat16),
            jax.ShapeDtypeStruct((QUARTER, BLOCK), jnp.bfloat16),
            jax.ShapeDtypeStruct((2 * QUARTER, BLOCK), jnp.bfloat16),
        ],
        scratch_shapes=[pltpu.VMEM((ROWS, tile), jnp.bfloat16)],
        cost_estimate=cost(2 * ROWS * WIDTH * BLOCK, 2 * WIDTH * BLOCK),
        name="encode",
    )(meta, rows, weight)


def decode_kernel(meta_ref, pair_ref, away_ref, weight_ref, out_ref, rows_ref):
    @pl.when(pl.program_id(0) == 0)
    def _():
        own, near, away, far = quarters(meta_ref)
        rows_ref[pl.ds(own, QUARTER), :] = pair_ref[0:QUARTER, :]
        rows_ref[pl.ds(near, QUARTER), :] = pair_ref[QUARTER:, :]
        rows_ref[pl.ds(away, QUARTER), :] = away_ref[0:QUARTER, :]
        rows_ref[pl.ds(far, QUARTER), :] = away_ref[QUARTER:, :]

    out_ref[...] = jnp.dot(rows_ref[...], weight_ref[...], preferred_element_type=jnp.float32).astype(jnp.bfloat16)


def decode(meta, pair, away, weight, tile=256):
    half = pl.BlockSpec((2 * QUARTER, BLOCK), lambda j: (0, 0))
    return pl.pallas_call(
        decode_kernel,
        grid=(WIDTH // tile,),
        in_specs=[smem(), half, half, pl.BlockSpec((BLOCK, tile), lambda j: (0, j))],
        out_specs=pl.BlockSpec((ROWS, tile), lambda j: (0, j)),
        out_shape=jax.ShapeDtypeStruct((ROWS, WIDTH), jnp.bfloat16),
        scratch_shapes=[pltpu.VMEM((ROWS, BLOCK), jnp.bfloat16)],
        cost_estimate=cost(2 * ROWS * WIDTH * BLOCK, 2 * WIDTH * BLOCK),
        name="decode",
    )(meta, pair, away, weight)


def collect(chunk, code_ref, rows_ref):
    return lax.dot_general(
        picks(code_ref, chunk), rows_ref[...], (((0,), (0,)), ((), ())), preferred_element_type=jnp.float32
    )


def collect_kernel(chunk, code_ref, rows_ref, base_ref, out_ref):
    out_ref[...] = base_ref[...] + collect(chunk, code_ref, rows_ref)


def collect_rows(chunk, code, rows, base):
    return pl.pallas_call(
        lambda *refs: collect_kernel(chunk, *refs),
        out_shape=jax.ShapeDtypeStruct((TOK, WIDTH), jnp.float32),
        cost_estimate=cost(2 * ROWS * TOK * WIDTH, 2 * ROWS * WIDTH),
        name="collect",
    )(code, rows, base)


def finish_kernel(chunk, act_ref, code_ref, rows_ref, base_ref, out_ref):
    recon = base_ref[...] + collect(chunk, code_ref, rows_ref)
    diff = act_ref[...].astype(jnp.float32) - recon
    out_ref[...] = lane_sums(diff * diff)


def finish(chunk, activations, code, rows, base):
    return pl.pallas_call(
        lambda *refs: finish_kernel(chunk, *refs),
        out_shape=jax.ShapeDtypeStruct((1, TOK), jnp.float32),
        cost_estimate=cost(2 * ROWS * TOK * WIDTH, 2 * ROWS * WIDTH),
        name="finish",
    )(activations, code, rows, base)


def sum_tp(value):
    value = value + send(value, TO_X1)
    return value + send(value, TO_X3)


def exchange(rows):
    rows = rows.reshape(OWNERS, PART, WIDTH)
    return lax.all_to_all(rows, "lat", split_axis=0, concat_axis=0, tiled=True).reshape(ROWS, WIDTH)


def body(activations, active_blocks, enc_weight, enc_bias, dec_weight, dec_bias):
    meta = (lax.axis_index("lat") * N_X + lax.axis_index("tp")).astype(jnp.int32).reshape(1)
    bias_row = dec_bias.reshape(1, WIDTH)
    code = codes(active_blocks.T)
    norms = sum_tp(norm_sums(activations)) + 1e-6

    def forward(chunk):
        rows = exchange(pack(chunk, activations, code, bias_row))
        own_part, near_part, away_part = encode(meta, rows, enc_weight)
        got = send(away_part, TO_XA)
        near_sum = (near_part.astype(jnp.float32) + got[QUARTER:].astype(jnp.float32)).astype(jnp.bfloat16)
        rest = send(near_sum, TO_XB)
        pre = own_part.astype(jnp.float32) + got[:QUARTER].astype(jnp.float32) + rest.astype(jnp.float32)
        mine = jnp.maximum(pre + enc_bias, 0.0).astype(jnp.bfloat16)
        near = send(mine, TO_XB)
        pair = jnp.concatenate([mine, near], axis=0)
        away = send(pair, TO_XA)
        return exchange(decode(meta, pair, away, dec_weight))

    back = [forward(chunk) for chunk in range(CHUNKS)]
    recon = bias_row
    for chunk in range(CHUNKS - 1):
        recon = collect_rows(chunk, code, back[chunk], recon)
    squares = sum_tp(finish(CHUNKS - 1, activations, code, back[-1], recon))
    token_error = (squares / norms).reshape(TOK)
    total = token_error[:128] + token_error[128:]
    for table in TO_LAT:
        total = total + send(total, table)
    mean_error = jnp.sum(total) / (TOK * OWNERS)
    return (token_error, mean_error)


def solution(mesh):
    in_specs = (P("lat", "tp"), P("lat", None), P("tp", "lat"), P("lat"), P("lat", "tp"), P("tp"))
    out_specs = (P("lat"), P())
    return jax.shard_map(body, mesh=mesh, in_specs=in_specs, out_specs=out_specs, check_vma=False)
```

```python
import jax
import jax.numpy as jnp
from jax import lax
from jax.experimental import pallas as pl
from jax.experimental.pallas import tpu as pltpu
from jax.sharding import PartitionSpec as P


AXES = ("lat", "tp")
N_Z, N_Y, N_C, N_X = 4, 4, 2, 4
OWNERS = N_Z * N_Y * N_C
TOK = 256
WIDTH = 1792
BLOCK = 2048
SLOTS = 32
CHUNKS = 2
PART = SLOTS // CHUNKS
ROWS = OWNERS * PART
QUARTER = ROWS // N_X


def split_index(index):
    x = index % N_X
    lat = index // N_X
    return lat // (N_Y * N_C), (lat // N_C) % N_Y, lat % N_C, x


def pairs(change):
    out = []
    for index in range(N_Z * N_Y * N_C * N_X):
        z, y, c, x = change(*split_index(index))
        out.append((index, ((z * N_Y + y) * N_C + c) * N_X + x))
    return out


def first(c):
    return 1 + 2 * c


def second(c):
    return 3 - 2 * c


TO_XA = pairs(lambda z, y, c, x: (z, y, c, x ^ first(c)))
TO_XB = pairs(lambda z, y, c, x: (z, y, c, x ^ second(c)))
TO_CORE = pairs(lambda z, y, c, x: (z, y, 1 - c, x))
TO_X = [pairs(lambda z, y, c, x, d=d: (z, y, c, x ^ d)) for d in (1, 2, 3)]
TO_Y = [pairs(lambda z, y, c, x, d=d: (z, y ^ d, c, x)) for d in (1, 2, 3)]
TO_Z = [pairs(lambda z, y, c, x, d=d: (z ^ d, y, c, x)) for d in (1, 2, 3)]


def send(value, table):
    return lax.ppermute(value, AXES, table)


def smem():
    return pl.BlockSpec(memory_space=pltpu.SMEM)


def whole():
    return pl.BlockSpec(memory_space=pltpu.VMEM)


def near_core(value):
    return pltpu.with_memory_space_constraint(value, pltpu.VMEM)


def call(kernel, outs, args, flops, local=(), scalars=0):
    moved = sum(a.size * a.dtype.itemsize for a in args) // 4
    args = [near_core(a) if i in local else a for i, a in enumerate(args)]
    return pl.pallas_call(
        kernel,
        in_specs=[smem()] * scalars + [whole()] * (len(args) - scalars),
        out_specs=[whole()] * len(outs),
        out_shape=[jax.ShapeDtypeStruct(shape, dtype) for shape, dtype in outs],
        cost_estimate=pl.CostEstimate(flops=flops, transcendentals=0, bytes_accessed=moved),
    )(*args)


def lane_sums(values):
    acc = values[:, :128]
    for start in range(128, values.shape[1], 128):
        acc = acc + values[:, start:start + 128]
    return jnp.sum(acc.T, axis=0, keepdims=True)


def code_kernel(ids_ref, code_ref):
    block = lax.broadcasted_iota(jnp.int32, (OWNERS, TOK), 0)
    one0 = jnp.where(ids_ref[0:1, :] == block, 1.0, 0.0)
    one1 = jnp.where(ids_ref[1:2, :] == block, 1.0, 0.0)
    before = lax.broadcasted_iota(jnp.int32, (TOK, TOK), 0) < lax.broadcasted_iota(jnp.int32, (TOK, TOK), 1)
    before = jnp.where(before, 1.0, 0.0).astype(jnp.bfloat16)
    count0 = jnp.dot(one0.astype(jnp.bfloat16), before, preferred_element_type=jnp.float32)
    count1 = jnp.dot(one1.astype(jnp.bfloat16), before, preferred_element_type=jnp.float32)
    count1 = count1 + jnp.sum(one0, axis=1, keepdims=True)
    rank0 = jnp.sum(one0 * count0, axis=0, keepdims=True)
    rank1 = jnp.sum(one1 * count1, axis=0, keepdims=True)
    code_ref[0:1, :] = ids_ref[0:1, :] * SLOTS + rank0.astype(jnp.int32)
    code_ref[1:2, :] = ids_ref[1:2, :] * SLOTS + rank1.astype(jnp.int32)


def codes(ids):
    return call(code_kernel, [((2, TOK), jnp.int32)], [ids], 2**24)[0]


def picks(code_ref, chunk):
    row = lax.broadcasted_iota(jnp.int32, (ROWS, 1), 0)
    want = row // PART * SLOTS + chunk * PART + row % PART
    hit = (code_ref[0:1, :] == want) | (code_ref[1:2, :] == want)
    return jnp.where(hit, 1.0, 0.0).astype(jnp.bfloat16)


def pack(chunk, activations, code, dec_bias):
    def kernel(act_ref, code_ref, bias_ref, out_ref):
        centred = (act_ref[...].astype(jnp.float32) - bias_ref[...]).astype(jnp.bfloat16)
        rows = jnp.dot(picks(code_ref, chunk), centred, preferred_element_type=jnp.float32)
        out_ref[...] = rows.astype(jnp.bfloat16).reshape(OWNERS, PART, WIDTH)

    return call(kernel, [((OWNERS, PART, WIDTH), jnp.bfloat16)], [activations, code, dec_bias], 2 * ROWS * TOK * WIDTH)[0]


def norm_sums(activations):
    def kernel(act_ref, out_ref):
        values = act_ref[...].astype(jnp.float32)
        out_ref[...] = lane_sums(values * values)

    return call(kernel, [((1, TOK), jnp.float32)], [activations], 2**20)[0]


def quarters(meta):
    index = meta[0]
    x, c = index % N_X, (index // N_X) % N_C
    return [pl.multiple_of((x ^ d) * QUARTER, QUARTER) for d in (0, second(c), first(c), 2)]


def encode(meta, rows, weight, tile=512):
    def kernel(meta_ref, rows_ref, weight_ref, own_ref, near_ref, away_ref, part_ref):
        own, near, away, far = quarters(meta_ref)
        part = jnp.dot(rows_ref[...].reshape(ROWS, WIDTH), weight_ref[...], preferred_element_type=jnp.float32)
        part_ref[...] = part.astype(jnp.bfloat16)
        own_ref[...] = part_ref[pl.ds(own, QUARTER), :]
        near_ref[...] = part_ref[pl.ds(near, QUARTER), :]
        away_ref[0:QUARTER, :] = part_ref[pl.ds(away, QUARTER), :]
        away_ref[QUARTER:, :] = part_ref[pl.ds(far, QUARTER), :]

    outs = [QUARTER, QUARTER, 2 * QUARTER]
    return pl.pallas_call(
        kernel,
        grid=(BLOCK // tile,),
        in_specs=[smem(), whole(), pl.BlockSpec((WIDTH, tile), lambda j: (0, j))],
        out_specs=[pl.BlockSpec((count, tile), lambda j: (0, j)) for count in outs],
        out_shape=[jax.ShapeDtypeStruct((count, BLOCK), jnp.bfloat16) for count in outs],
        scratch_shapes=[pltpu.VMEM((ROWS, tile), jnp.bfloat16)],
        cost_estimate=pl.CostEstimate(flops=2 * ROWS * WIDTH * BLOCK, transcendentals=0, bytes_accessed=2 * WIDTH * BLOCK),
        name="encode",
    )(meta, near_core(rows), weight)


def join(near_part, got):
    def kernel(near_ref, got_ref, out_ref):
        total = near_ref[...].astype(jnp.float32) + got_ref[QUARTER:, :].astype(jnp.float32)
        out_ref[...] = total.astype(jnp.bfloat16)

    return call(kernel, [((QUARTER, BLOCK), jnp.bfloat16)], [near_part, got], 2**18, local=(1,))[0]


def activate(own_part, got, rest, enc_bias):
    def kernel(own_ref, got_ref, rest_ref, bias_ref, out_ref):
        pre = own_ref[...].astype(jnp.float32) + got_ref[0:QUARTER, :].astype(jnp.float32)
        pre = pre + rest_ref[...].astype(jnp.float32) + bias_ref[...]
        out_ref[...] = jnp.maximum(pre, 0.0).astype(jnp.bfloat16)

    return call(kernel, [((QUARTER, BLOCK), jnp.bfloat16)], [own_part, got, rest, enc_bias], 2**19, local=(1, 2))[0]


def decode(meta, own, others, weight, tile=256):
    def kernel(meta_ref, own_ref, near_ref, away_ref, far_ref, weight_ref, out_ref, rows_ref):
        @pl.when(pl.program_id(0) == 0)
        def _():
            for start, part_ref in zip(quarters(meta_ref), (own_ref, near_ref, away_ref, far_ref)):
                rows_ref[pl.ds(start, QUARTER), :] = part_ref[...]

        rows = jnp.dot(rows_ref[...], weight_ref[...], preferred_element_type=jnp.float32)
        out_ref[...] = rows.astype(jnp.bfloat16).reshape(OWNERS, PART, tile)

    return pl.pallas_call(
        kernel,
        grid=(WIDTH // tile,),
        in_specs=[smem()] + [whole()] * 4 + [pl.BlockSpec((BLOCK, tile), lambda j: (0, j))],
        out_specs=pl.BlockSpec((OWNERS, PART, tile), lambda j: (0, 0, j)),
        out_shape=jax.ShapeDtypeStruct((OWNERS, PART, WIDTH), jnp.bfloat16),
        scratch_shapes=[pltpu.VMEM((ROWS, BLOCK), jnp.bfloat16)],
        cost_estimate=pl.CostEstimate(flops=2 * ROWS * WIDTH * BLOCK, transcendentals=0, bytes_accessed=2 * WIDTH * BLOCK),
        name="decode",
    )(meta, own, *[near_core(a) for a in others], weight)


def collect(chunk, code_ref, rows_ref):
    return lax.dot_general(
        picks(code_ref, chunk), rows_ref[...].reshape(ROWS, WIDTH), (((0,), (0,)), ((), ())), preferred_element_type=jnp.float32
    )


def collect_rows(chunk, code, rows, base):
    def kernel(code_ref, rows_ref, base_ref, out_ref):
        out_ref[...] = base_ref[...] + collect(chunk, code_ref, rows_ref)

    return call(kernel, [((TOK, WIDTH), jnp.float32)], [code, rows, base], 2 * ROWS * TOK * WIDTH)[0]


def finish(chunk, activations, code, rows, base):
    def kernel(act_ref, code_ref, rows_ref, base_ref, out_ref):
        recon = base_ref[...] + collect(chunk, code_ref, rows_ref)
        diff = act_ref[...].astype(jnp.float32) - recon
        out_ref[...] = lane_sums(diff * diff)

    return call(kernel, [((1, TOK), jnp.float32)], [activations, code, rows, base], 2 * ROWS * TOK * WIDTH, local=(2,))[0]


def sum_tp(value):
    one, two, three = (send(value, table) for table in TO_X)
    return (value + two) + (one + three)


def exchange(rows):
    return lax.all_to_all(rows, "lat", split_axis=0, concat_axis=0, tiled=True)


def steps(activations, active_blocks, enc_weight, enc_bias, dec_weight, dec_bias):
    meta = (lax.axis_index("lat") * N_X + lax.axis_index("tp")).astype(jnp.int32).reshape(1)
    bias_row = dec_bias.reshape(1, WIDTH)
    code = codes(active_blocks.T)

    def forward(n):
        rows = pack(n, activations, code, bias_row)
        rows = exchange(rows)
        own_part, near_part, away_part = encode(meta, rows, enc_weight)
        got = send(away_part, TO_XA)
        near_sum = join(near_part, got)
        rest = send(near_sum, TO_XB)
        mine = activate(own_part, got, rest, enc_bias.reshape(1, BLOCK))
        near = send(mine, TO_XB)
        away = send(mine, TO_XA)
        far = send(near, TO_XA)
        rows = decode(meta, mine, (near, away, far), dec_weight)
        return exchange(rows)

    back = [forward(n) for n in range(CHUNKS)]
    norms = sum_tp(norm_sums(activations)) + 1e-6
    recon = bias_row
    for n in range(CHUNKS - 1):
        recon = collect_rows(n, code, back[n], recon)
    partial = finish(CHUNKS - 1, activations, code, back[-1], recon)
    squares = sum_tp(partial)
    token_error = (squares / norms).reshape(TOK)
    total = token_error[:128] + token_error[128:]
    total = total + send(total, TO_CORE)
    for tables in (TO_Y, TO_Z):
        one, two, three = (send(total, table) for table in tables)
        total = (total + two) + (one + three)
    mean_error = jnp.sum(total) / (TOK * OWNERS)
    return (token_error, mean_error)


def solution(mesh):
    in_specs = (P("lat", "tp"), P("lat", None), P("tp", "lat"), P("lat"), P("lat", "tp"), P("tp"))
    out_specs = (P("lat"), P())
    return jax.shard_map(steps, mesh=mesh, in_specs=in_specs, out_specs=out_specs, check_vma=False)
```

```python
import jax
import jax.numpy as jnp
from jax import lax
from jax.experimental import pallas as pl
from jax.experimental.pallas import tpu as pltpu
from jax.sharding import PartitionSpec as P


AXES = ("lat", "tp")
N_Z, N_Y, N_C, N_X = 4, 4, 2, 4
OWNERS = N_Z * N_Y * N_C
TOK = 256
WIDTH = 1792
BLOCK = 2048
SLOTS = 32
CHUNKS = 2
PART = SLOTS // CHUNKS
ROWS = OWNERS * PART
QUARTER = ROWS // N_X
HALVES = 2


def split_index(index):
    x = index % N_X
    lat = index // N_X
    return lat // (N_Y * N_C), (lat // N_C) % N_Y, lat % N_C, x


def pairs(change):
    out = []
    for index in range(N_Z * N_Y * N_C * N_X):
        z, y, c, x = change(*split_index(index))
        out.append((index, ((z * N_Y + y) * N_C + c) * N_X + x))
    return out


def first(c):
    return 1 + 2 * c


def second(c):
    return 3 - 2 * c


TO_XA = pairs(lambda z, y, c, x: (z, y, c, x ^ first(c)))
TO_XB = pairs(lambda z, y, c, x: (z, y, c, x ^ second(c)))
TO_CORE = pairs(lambda z, y, c, x: (z, y, 1 - c, x))
TO_X = [pairs(lambda z, y, c, x, d=d: (z, y, c, x ^ d)) for d in (1, 2, 3)]
TO_Y = [pairs(lambda z, y, c, x, d=d: (z, y ^ d, c, x)) for d in (1, 2, 3)]
TO_Z = [pairs(lambda z, y, c, x, d=d: (z ^ d, y, c, x)) for d in (1, 2, 3)]


def send(value, table):
    return lax.ppermute(value, AXES, table)


def smem():
    return pl.BlockSpec(memory_space=pltpu.SMEM)


def whole():
    return pl.BlockSpec(memory_space=pltpu.VMEM)


def near_core(value):
    return pltpu.with_memory_space_constraint(value, pltpu.VMEM)


def call(kernel, outs, args, flops, local=(), scalars=0):
    moved = sum(a.size * a.dtype.itemsize for a in args) // 4
    args = [near_core(a) if i in local else a for i, a in enumerate(args)]
    return pl.pallas_call(
        kernel,
        in_specs=[smem()] * scalars + [whole()] * (len(args) - scalars),
        out_specs=[whole()] * len(outs),
        out_shape=[jax.ShapeDtypeStruct(shape, dtype) for shape, dtype in outs],
        cost_estimate=pl.CostEstimate(flops=flops, transcendentals=0, bytes_accessed=moved),
    )(*args)


def lane_sums(values):
    acc = values[:, :128]
    for start in range(128, values.shape[1], 128):
        acc = acc + values[:, start:start + 128]
    return jnp.sum(acc.T, axis=0, keepdims=True)


def slot_codes(ids_ref):
    block = lax.broadcasted_iota(jnp.int32, (OWNERS, TOK), 0)
    one0 = jnp.where(ids_ref[0:1, :] == block, 1.0, 0.0)
    one1 = jnp.where(ids_ref[1:2, :] == block, 1.0, 0.0)
    before = lax.broadcasted_iota(jnp.int32, (TOK, TOK), 0) < lax.broadcasted_iota(jnp.int32, (TOK, TOK), 1)
    before = jnp.where(before, 1.0, 0.0).astype(jnp.bfloat16)
    count0 = jnp.dot(one0.astype(jnp.bfloat16), before, preferred_element_type=jnp.float32)
    count1 = jnp.dot(one1.astype(jnp.bfloat16), before, preferred_element_type=jnp.float32)
    count1 = count1 + jnp.sum(one0, axis=1, keepdims=True)
    rank0 = jnp.sum(one0 * count0, axis=0, keepdims=True).astype(jnp.int32)
    rank1 = jnp.sum(one1 * count1, axis=0, keepdims=True).astype(jnp.int32)
    return ids_ref[0:1, :] * SLOTS + rank0, ids_ref[1:2, :] * SLOTS + rank1


def picks(code0, code1, chunk):
    row = lax.broadcasted_iota(jnp.int32, (ROWS, 1), 0)
    want = row // PART * SLOTS + chunk * PART + row % PART
    hit = (code0 == want) | (code1 == want)
    return jnp.where(hit, 1.0, 0.0).astype(jnp.bfloat16)


def packed_rows(values, code0, code1, bias_ref, chunk):
    centred = (values - bias_ref[...].reshape(1, WIDTH)).astype(jnp.bfloat16)
    rows = jnp.dot(picks(code0, code1, chunk), centred, preferred_element_type=jnp.float32)
    return rows.astype(jnp.bfloat16).reshape(OWNERS, PART, WIDTH)


def pack_first(activations, ids, dec_bias):
    def kernel(act_ref, ids_ref, bias_ref, code_ref, out_ref):
        code0, code1 = slot_codes(ids_ref)
        code_ref[0:1, :] = code0
        code_ref[1:2, :] = code1
        out_ref[...] = packed_rows(act_ref[...].astype(jnp.float32), code0, code1, bias_ref, 0)

    outs = [((2, TOK), jnp.int32), ((OWNERS, PART, WIDTH), jnp.bfloat16)]
    return call(kernel, outs, [activations, ids, dec_bias], 2 * ROWS * TOK * WIDTH)


def pack_next(chunk, activations, code, dec_bias):
    def kernel(act_ref, code_ref, bias_ref, out_ref, norm_ref):
        values = act_ref[...].astype(jnp.float32)
        norm_ref[...] = lane_sums(values * values)
        out_ref[...] = packed_rows(values, code_ref[0:1, :], code_ref[1:2, :], bias_ref, chunk)

    outs = [((OWNERS, PART, WIDTH), jnp.bfloat16), ((1, TOK), jnp.float32)]
    return call(kernel, outs, [activations, code, dec_bias], 2 * ROWS * TOK * WIDTH)


def quarters(meta):
    index = meta[0]
    x, c = index % N_X, (index // N_X) % N_C
    return [pl.multiple_of((x ^ d) * QUARTER, QUARTER) for d in (0, second(c), first(c), 2)]


def encode(half, meta, rows, weight, bias, tile=512):
    steps = BLOCK // HALVES // tile

    def kernel(meta_ref, rows_ref, weight_ref, bias_ref, own_ref, near_ref, away_ref, part_ref):
        own, near, away, far = quarters(meta_ref)
        part = jnp.dot(rows_ref[...].reshape(ROWS, WIDTH), weight_ref[...], preferred_element_type=jnp.float32)
        part_ref[...] = part.astype(jnp.bfloat16)
        own_ref[...] = part_ref[pl.ds(own, QUARTER), :].astype(jnp.float32) + bias_ref[...]
        near_ref[...] = part_ref[pl.ds(near, QUARTER), :]
        away_ref[0:QUARTER, :] = part_ref[pl.ds(away, QUARTER), :]
        away_ref[QUARTER:, :] = part_ref[pl.ds(far, QUARTER), :]

    outs = [(QUARTER, jnp.float32), (QUARTER, jnp.bfloat16), (2 * QUARTER, jnp.bfloat16)]
    wide = BLOCK // HALVES
    return pl.pallas_call(
        kernel,
        grid=(steps,),
        in_specs=[
            smem(),
            whole(),
            pl.BlockSpec((WIDTH, tile), lambda j: (0, half * steps + j)),
            pl.BlockSpec((1, tile), lambda j: (0, half * steps + j)),
        ],
        out_specs=[pl.BlockSpec((count, tile), lambda j: (0, j)) for count, _ in outs],
        out_shape=[jax.ShapeDtypeStruct((count, wide), dtype) for count, dtype in outs],
        scratch_shapes=[pltpu.VMEM((ROWS, tile), jnp.bfloat16)],
        cost_estimate=pl.CostEstimate(flops=2 * ROWS * WIDTH * wide, transcendentals=0, bytes_accessed=2 * WIDTH * wide),
        name="encode",
    )(meta, near_core(rows), weight, bias)


def decode(meta, parts, weight, tile=896):
    wide = BLOCK // HALVES

    def kernel(meta_ref, *refs):
        weight_ref, out_ref, rows_ref = refs[4 * HALVES:]

        @pl.when(pl.program_id(0) == 0)
        def _():
            for half in range(HALVES):
                for start, part_ref in zip(quarters(meta_ref), refs[4 * half:4 * half + 4]):
                    rows_ref[pl.ds(start, QUARTER), half * wide:(half + 1) * wide] = part_ref[...]

        rows = jnp.dot(rows_ref[...], weight_ref[...], preferred_element_type=jnp.float32)
        out_ref[...] = rows.astype(jnp.bfloat16).reshape(OWNERS, PART, tile)

    args = []
    for own, *others in parts:
        args += [own] + [near_core(a) for a in others]
    return pl.pallas_call(
        kernel,
        grid=(WIDTH // tile,),
        in_specs=[smem()] + [whole()] * (4 * HALVES) + [pl.BlockSpec((BLOCK, tile), lambda j: (0, j))],
        out_specs=pl.BlockSpec((OWNERS, PART, tile), lambda j: (0, 0, j)),
        out_shape=jax.ShapeDtypeStruct((OWNERS, PART, WIDTH), jnp.bfloat16),
        scratch_shapes=[pltpu.VMEM((ROWS, BLOCK), jnp.bfloat16)],
        cost_estimate=pl.CostEstimate(flops=2 * ROWS * WIDTH * BLOCK, transcendentals=0, bytes_accessed=2 * WIDTH * BLOCK),
        name="decode",
    )(meta, *args, weight)


def collect(chunk, code_ref, rows_ref):
    return lax.dot_general(
        picks(code_ref[0:1, :], code_ref[1:2, :], chunk), rows_ref[...].reshape(ROWS, WIDTH), (((0,), (0,)), ((), ())), preferred_element_type=jnp.float32
    )


def collect_rows(chunk, code, rows, base):
    def kernel(code_ref, rows_ref, base_ref, out_ref):
        out_ref[...] = base_ref[...].reshape(-1, WIDTH) + collect(chunk, code_ref, rows_ref)

    return call(kernel, [((TOK, WIDTH), jnp.float32)], [code, rows, base], 2 * ROWS * TOK * WIDTH)[0]


def finish(chunk, activations, code, rows, base):
    def kernel(act_ref, code_ref, rows_ref, base_ref, out_ref):
        recon = base_ref[...] + collect(chunk, code_ref, rows_ref)
        diff = act_ref[...].astype(jnp.float32) - recon
        out_ref[...] = lane_sums(diff * diff)

    return call(kernel, [((1, TOK), jnp.float32)], [activations, code, rows, base], 2 * ROWS * TOK * WIDTH, local=(2,))[0]


def sum_tp(value):
    one, two, three = (send(value, table) for table in TO_X)
    return (value + two) + (one + three)


def exchange(rows):
    return lax.all_to_all(rows, "lat", split_axis=0, concat_axis=0, tiled=True)


def steps(activations, active_blocks, enc_weight, enc_bias, dec_weight, dec_bias):
    meta = (lax.axis_index("lat") * N_X + lax.axis_index("tp")).astype(jnp.int32).reshape(1)
    enc_row = enc_bias.reshape(1, BLOCK)
    code, first_rows = pack_first(activations, active_blocks.T, dec_bias)
    sent, norm = [first_rows], None
    for n in range(1, CHUNKS):
        rows, norm = pack_next(n, activations, code, dec_bias)
        sent.append(rows)

    def share(half, rows):
        own_part, near_part, away_part = encode(half, meta, rows, enc_weight, enc_row)
        got = send(away_part, TO_XA)
        near_sum = (near_part.astype(jnp.float32) + got[QUARTER:].astype(jnp.float32)).astype(jnp.bfloat16)
        rest = send(near_sum, TO_XB)
        pre = own_part + got[:QUARTER].astype(jnp.float32) + rest.astype(jnp.float32)
        mine = jnp.maximum(pre, 0.0).astype(jnp.bfloat16)
        near = send(mine, TO_XB)
        away = send(mine, TO_XA)
        far = send(near, TO_XA)
        return mine, near, away, far

    back = []
    for n in range(CHUNKS):
        rows = exchange(sent[n])
        parts = [share(half, rows) for half in range(HALVES)]
        rows = decode(meta, parts, dec_weight)
        back.append(exchange(rows))

    norms = sum_tp(norm) + 1e-6
    recon = dec_bias
    for n in range(CHUNKS - 1):
        recon = collect_rows(n, code, back[n], recon)
    partial = finish(CHUNKS - 1, activations, code, back[-1], recon)
    squares = sum_tp(partial)
    token_error = (squares / norms).reshape(TOK)
    total = token_error[:128] + token_error[128:]
    total = total + send(total, TO_CORE)
    for tables in (TO_Y, TO_Z):
        one, two, three = (send(total, table) for table in tables)
        total = (total + two) + (one + three)
    mean_error = jnp.sum(total) / (TOK * OWNERS)
    return (token_error, mean_error)


def solution(mesh):
    in_specs = (P("lat", "tp"), P("lat", None), P("tp", "lat"), P("lat"), P("lat", "tp"), P("tp"))
    out_specs = (P("lat"), P())
    return jax.shard_map(steps, mesh=mesh, in_specs=in_specs, out_specs=out_specs, check_vma=False)
```
